256 devices in a mesh: dom: 64 (over x, z, y_lo), feat: 4 (over y_hi, core).
Axes of the slice: x: 4, y: 4 (y_hi: 2, y_lo: 2; y = y_hi * 2 + y_lo), z: 8, core: 2. Of those that a mesh axis runs over, the one named last changes fastest.
Arguments:
- embed: bfloat16 [256, 65536], P('feat', 'dom'), may hold values from -6 to 6
- weight: bfloat16 [256, 256], P('feat'), may hold values from -0.375 to 0.375
- cotangent: bfloat16 [256, 65536], P('feat', 'dom'), may hold values from -6 to 6
- edge_masks: int32 [6144, 128, 128], P('dom'), may hold values 0 or 1
- tile_rows: int32 [6144], P('dom'), may hold values from 0 to 7
- tile_owner: int32 [6144, 1], P('dom'), may hold values from 0 to 63; in each aligned block of 96 rows (0 to 95, 96 to 191, ...) at most 2 rows name the same one
- tile_sub: int32 [6144], P('dom'), may hold values from 0 to 7
Outputs:
- output: bfloat16 [256, 65536], P('feat', 'dom')
- embed_grad: float32 [256, 65536], P('feat', 'dom')
- weight_grad: float32 [256, 256], P('feat')
The draws below stay inside these ranges and needn't reach their ends.
Inputs may be any that keep to these rules, and one draw needn't show every extreme that they name: `tile_owner`: among the 96 tiles of one index of dom no owner is named more than 2 times, a bound that some block reaches.
All inputs are finite; a program needn't handle non-finite values. No bound on the sum of `edge_masks` on one device may be relied on, other than what follows from the above.
Results may differ from the reference program's by a relative error of at most 0.0059.
Values may be sent and summed in bfloat16 or wider, within the bound.
No kernel may reach another device: no remote copies, remote signals or barrier semaphores. Data moves between devices by JAX's collectives and lax.ppermute only.
A program may use at most 64 MiB of HBM per device.

```python
import math
import jax
import jax.numpy as jnp
import numpy as np
from jax import lax

H = 256
BLK = 128
NB_DEV = 8
TILES_DEV = 96
TILES = 6144
NBLK = 512
NODES = 65536
CAP = 2
N_DOM = 64


def place_ends(values, stream_key, low, high):
    extent = values.shape
    spot = [jax.random.randint(jax.random.fold_in(stream_key, axis), (), 0, extent[axis]) for axis in range(len(extent))]
    values = values.at[tuple(spot)].set(low)
    longest = extent.index(max(extent))
    spot[longest] = (spot[longest] + 1) % extent[longest]
    return values.at[tuple(spot)].set(high)


def level_of(own_key, shape, split, least, top_value):
    gain = 1.0
    for position, blocks in split:
        draws = jax.random.uniform(jax.random.fold_in(jax.random.fold_in(own_key, 6), position), (blocks,), jnp.float32, least / len(split), top_value / len(split))
        gain = gain * jnp.repeat(jnp.exp(draws), shape[position] // blocks).reshape((-1,) + (1,) * (len(shape) - 1 - position))
    return gain


def shared_out(rng, own, number, rows, amount, top, bound, skew):
    sequence = jax.random.permutation(rng, amount)
    crowded, common = load_shares(amount, rows * top, bound, skew, True), load_shares(amount, rows * top, bound, skew, False)
    places = jnp.arange(amount)

    def named(lengths, turn):
        used = int((lengths > 0).sum())
        fixed = max(1, used // 4)
        passed = fixed + (places - fixed + turn * (used - fixed)) % max(1, amount - fixed)
        return jnp.zeros((amount,), jnp.int32).at[sequence[jnp.where(places < fixed, places, passed)]].set(jnp.asarray(lengths, jnp.int32))

    lengths = jnp.where(number % 4 == 0, named(crowded, number // 4), named(common, number - number // 4 - 1))
    mixed = jax.random.permutation(jax.random.fold_in(own, 3), amount)
    donor, receiver = mixed[0:amount // 2 * 2:2], mixed[1:amount // 2 * 2:2]
    slack = jnp.minimum(lengths[donor] - 1, bound - lengths[receiver]) // 2
    slack = jnp.where((donor == sequence[0]) | (receiver == sequence[0]) | (lengths[receiver] == 0), 0, jnp.maximum(slack, 0))
    passed = jax.random.randint(jax.random.fold_in(own, 4), (amount // 2,), 0, 1 << 20) % (slack + 1)
    lengths = lengths.at[donor].add(-passed).at[receiver].add(passed)
    items = jnp.searchsorted(jnp.cumsum(lengths), jnp.arange(rows * top), side="right").astype(jnp.int32)
    table = items.reshape(top, rows).T
    table = table[jax.random.permutation(jax.random.fold_in(own, 1), rows)]
    turn = jax.random.randint(jax.random.fold_in(own, 2), (rows, 1), 0, top)
    return jnp.take_along_axis(table, (jnp.arange(top)[None, :] + turn) % top, axis=1)


def load_shares(amount, total, most, skew, full):
    portions = [(1 << 20) // math.isqrt(grade ** skew) + 1 for grade in range(1, amount + 1)]
    largest = most if full else min(most, max(-(-total // amount), total * portions[0] // sum(portions)))
    least = 1 if total - largest >= amount - 1 else 0
    given, spare = [largest] + [least] * (amount - 1), total - largest - least * (amount - 1)
    while spare > 0:
        candidates = [i for i in range(1, amount) if given[i] < largest] or [i for i in range(1, amount) if given[i] < most]
        whole, left = sum([portions[i] for i in candidates]), spare
        for i in candidates:
            extra = min(most - given[i], max(1, left * portions[i] // whole), spare)
            given[i] = given[i] + extra
            spare = spare - extra
    return np.array(given)


def gaussian(key, extent, deviation, limit, split=(), kind=jnp.bfloat16):
    drawn = jax.random.normal(key, extent, jnp.float32) * deviation
    if len(split) > 0:
        drawn = level_of(key, extent, split, -0.22, 0.18) * drawn
    return jnp.clip(drawn, min=-limit, max=limit).astype(kind)


def setup_inputs(seed: int = 0) -> dict:
    arg_keys = jax.random.split(jax.random.key(seed), 8)
    embed = gaussian(arg_keys[0], (H, NODES), 1.0, 6.0, ((0, 4), (1, 64)))
    weight = gaussian(arg_keys[1], (H, H), H ** -0.5, 0.375, ((0, 4),))
    cotangent = gaussian(arg_keys[2], (H, NODES), 1.0, 6.0, ((0, 4), (1, 64)))
    edge_masks = place_ends((jax.random.randint(arg_keys[3], (TILES, BLK, BLK), 0, 16) < 1).astype(jnp.int32), jax.random.fold_in(arg_keys[3], 1), 0, 1)
    tile_rows = place_ends(jax.random.randint(arg_keys[4], (TILES,), 0, NB_DEV), jax.random.fold_in(arg_keys[4], 1), 0, NB_DEV - 1).astype(jnp.int32)
    tile_owner_keys = jax.random.split(jax.random.fold_in(arg_keys[5], 1), TILES // TILES_DEV)
    tile_owner_turns = jax.random.permutation(jax.random.fold_in(arg_keys[5], 3), TILES // TILES_DEV)
    tile_owner = jax.vmap(lambda own, number: shared_out(jax.random.fold_in(arg_keys[5], 2), own, number, TILES_DEV, N_DOM, 1, CAP, 2))(tile_owner_keys, tile_owner_turns).reshape((TILES, 1))
    tile_sub = place_ends(jax.random.randint(arg_keys[6], (TILES,), 0, NB_DEV), jax.random.fold_in(arg_keys[6], 1), 0, NB_DEV - 1).astype(jnp.int32)
    return {"embed": embed, "weight": weight, "cotangent": cotangent, "edge_masks": edge_masks, "tile_rows": tile_rows, "tile_owner": tile_owner, "tile_sub": tile_sub}


def reference(embed, weight, cotangent, edge_masks, tile_rows, tile_owner, tile_sub):
    blocks = embed.reshape(H, NBLK, BLK)
    tile_masks = edge_masks.reshape(N_DOM, TILES_DEV, BLK, BLK)
    row_ids = tile_rows.reshape(N_DOM, TILES_DEV).astype(jnp.int32)
    col_ids = (tile_owner[:, 0] * NB_DEV + tile_sub).astype(jnp.int32).reshape(N_DOM, TILES_DEV)
    block_range = jnp.arange(NB_DEV, dtype=jnp.int32)

    def forward_block(packed):
        mask_one, row_one, col_one = packed
        fetched = jnp.take(blocks, col_one, axis=1).astype(jnp.float32)
        contrib = jnp.einsum('htj,tij->hti', fetched, mask_one.astype(jnp.float32))
        row_onehot = (row_one[:, None] == block_range[None, :]).astype(jnp.float32)
        neighbour = jnp.einsum('hti,tr->hri', contrib, row_onehot, precision=lax.Precision.HIGHEST)
        row_int = (row_one[:, None] == block_range[None, :]).astype(jnp.int32)
        counts = lax.optimization_barrier(jnp.sum(mask_one, axis=2)).astype(jnp.int32)
        degree = jnp.dot(row_int.T, counts)
        inv_root = 1.0 / jnp.sqrt(1.0 + degree.astype(jnp.float32))
        return (neighbour, inv_root)
    neighbours, roots = lax.map(forward_block, (tile_masks, row_ids, col_ids))
    neighbour = jnp.transpose(neighbours, (1, 0, 2, 3)).reshape(H, NODES)
    inv_root = roots.reshape(NODES)
    aggregate = (embed.astype(jnp.float32) + neighbour * inv_root[None, :]).astype(jnp.bfloat16)
    pre_act = jnp.dot(weight.T, aggregate, preferred_element_type=jnp.float32)
    gate_vals = jax.nn.sigmoid(pre_act)
    output = (pre_act * gate_vals).astype(jnp.bfloat16)
    grad_pre = (cotangent.astype(jnp.float32) * gate_vals * (1.0 + pre_act * (1.0 - gate_vals))).astype(jnp.bfloat16)
    grad_agg = jnp.dot(weight, grad_pre, preferred_element_type=jnp.float32)
    weight_grad = jnp.dot(aggregate, grad_pre.T, preferred_element_type=jnp.float32) / math.sqrt(NODES)
    scaled_grad = (grad_agg * inv_root[None, :]).astype(jnp.bfloat16)
    scaled_parts = jnp.transpose(scaled_grad.reshape(H, N_DOM, NB_DEV, BLK), (1, 0, 2, 3))

    def backward_block(totals, packed):
        mask_one, row_one, col_one, grad_part = packed
        selected = jnp.take(grad_part, row_one, axis=1).astype(jnp.float32)
        partial_value = jnp.einsum('hti,tij->htj', selected, mask_one.astype(jnp.float32))
        totals = totals.at[:, col_one].add(partial_value)
        return (totals, None)
    start_totals = jnp.zeros((H, NBLK, BLK), jnp.float32)
    totals, unused = lax.scan(backward_block, start_totals, (tile_masks, row_ids, col_ids, scaled_parts))
    embed_grad = grad_agg + totals.reshape(H, NODES)
    return (output, embed_grad, weight_grad)
```

```python
import functools
import math

import jax
import jax.numpy as jnp
from jax import lax
from jax.experimental import pallas as pl
from jax.experimental.pallas import tpu as pltpu
from jax.sharding import PartitionSpec as P

F32 = jnp.float32
BF16 = jnp.bfloat16
VM = pl.BlockSpec(memory_space=pltpu.VMEM)
SM = pl.BlockSpec(memory_space=pltpu.SMEM)


def params(mib):
    return pltpu.CompilerParams(vmem_limit_bytes=mib << 20)


def cost(flops, moved, exps=0):
    return pl.CostEstimate(flops=flops, bytes_accessed=moved, transcendentals=exps)


def slots_kernel(owner_ref, sub_ref, ask_ref, slot_ref):
    owners = ask_ref.shape[0]
    tiles = owner_ref.shape[1]
    ids = lax.broadcasted_iota(jnp.int32, (owners, tiles), 0)
    hit = ids == owner_ref[...]
    earlier = lax.broadcasted_iota(jnp.int32, (tiles, tiles), 0) < lax.broadcasted_iota(
        jnp.int32, (tiles, tiles), 1
    )
    before = jnp.dot(
        hit.astype(F32).astype(BF16), earlier.astype(F32).astype(BF16), preferred_element_type=F32
    )
    sub = sub_ref[...].astype(F32)
    first = jnp.sum(jnp.where(hit & (before < 0.5), sub, 0.0), axis=1, keepdims=True)
    second = jnp.sum(jnp.where(hit & (before > 0.5), sub, 0.0), axis=1, keepdims=True)
    lane = lax.broadcasted_iota(jnp.int32, ask_ref.shape, 1)
    ask_ref[...] = jnp.where(lane == 0, first, jnp.where(lane == 1, second, 0.0)).astype(jnp.int32)
    slot_ref[...] = jnp.sum(
        jnp.where(hit, 2.0 * ids.astype(F32) + before, 0.0), axis=0, keepdims=True
    ).astype(jnp.int32)


def select_kernel(want_ref, own_ref, send_ref):
    readers = want_ref.shape[0]
    width = send_ref.shape[2]

    def body(step, carry):
        for j in range(8):
            reader = step * 8 + j
            for k in range(2):
                start = pl.multiple_of(want_ref[reader, k] * width, width)
                send_ref[reader * 2 + k] = own_ref[:, pl.ds(start, width)]
        return carry

    lax.fori_loop(0, readers // 8, body, 0)


def masks_kernel(rows_ref, edge_ref, mask_ref, root_ref, degree_ref):
    step = pl.program_id(0)
    many = edge_ref.shape[0]

    @pl.when(step == 0)
    def _():
        degree_ref[...] = jnp.zeros_like(degree_ref)

    ones = jnp.ones((8, edge_ref.shape[2]), BF16)
    for j in range(many):
        mask = edge_ref[j].astype(F32).astype(BF16)
        mask_ref[j] = mask
        count = lax.dot_general(ones, mask, (((1,), (1,)), ((), ())), preferred_element_type=F32)
        row = rows_ref[step * many + j]
        degree_ref[row] = degree_ref[row] + count

    @pl.when(step == pl.num_programs(0) - 1)
    def _():
        root_ref[...] = 1.0 / jnp.sqrt(1.0 + degree_ref[...])


def forward_kernel(slot_ref, rows_ref, got_ref, mask_ref, own_ref, root_ref, agg_ref, acc_ref):
    tiles = mask_ref.shape[0]
    blocks, _, width = acc_ref.shape
    acc_ref[...] = jnp.zeros_like(acc_ref)
    group = 8

    def body(step, carry):
        terms = []
        for j in range(group):
            tile = step * group + j
            terms.append(
                lax.dot_general(
                    got_ref[slot_ref[tile]],
                    mask_ref[tile],
                    (((1,), (1,)), ((), ())),
                    preferred_element_type=F32,
                )
            )
        for j in range(group):
            row = rows_ref[step * group + j]
            acc_ref[row] = acc_ref[row] + terms[j]
        return carry

    lax.fori_loop(0, tiles // group, body, 0)
    for r in range(blocks):
        cols = slice(r * width, (r + 1) * width)
        agg_ref[:, cols] = (
            own_ref[:, cols].astype(F32) + acc_ref[r] * root_ref[r, 0:1, :]
        ).astype(BF16)


def dense_kernel(
    part_ref, agg_ref, aggown_ref, full_ref, weight_ref, root_ref,
    out_ref, grad_ref, scaled_ref, terms_ref, act_ref,
):
    nodes = agg_ref.shape[1]
    feats = weight_ref.shape[0]
    width = scaled_ref.shape[2]
    first = pl.multiple_of(part_ref[0] * feats, feats)
    chunk = 2 * width
    terms = jnp.zeros(terms_ref.shape, F32)
    for c in range(nodes // chunk):
        cols = slice(c * chunk, (c + 1) * chunk)
        pre = lax.dot_general(
            full_ref[:, nodes:], agg_ref[:, cols], (((0,), (0,)), ((), ())), preferred_element_type=F32
        )
        gate = jax.nn.sigmoid(pre)
        act_ref[...] = pre * gate
        out_ref[:, cols] = act_ref[pl.ds(first, feats), :].astype(BF16)
        grad_pre = (full_ref[:, cols].astype(F32) * gate * (1.0 + pre * (1.0 - gate))).astype(BF16)
        grad = jnp.dot(weight_ref[...], grad_pre, preferred_element_type=F32)
        grad_ref[:, cols] = grad
        terms = terms + lax.dot_general(
            aggown_ref[:, cols], grad_pre, (((1,), (1,)), ((), ())), preferred_element_type=F32
        )
        for k in range(2):
            r = 2 * c + k
            scaled_ref[r] = (grad[:, k * width:(k + 1) * width] * root_ref[r, 0:1, :]).astype(BF16)
    terms_ref[...] = terms


def backward_kernel(slot_ref, rows_ref, scaled_ref, mask_ref, send_ref):
    tiles = mask_ref.shape[0]
    group = 8
    send_ref[...] = jnp.zeros_like(send_ref)

    def body(step, carry):
        for j in range(group):
            tile = step * group + j
            send_ref[slot_ref[tile]] = jnp.dot(
                scaled_ref[rows_ref[tile]], mask_ref[tile], preferred_element_type=F32
            ).astype(BF16)
        return carry

    lax.fori_loop(0, tiles // group, body, 0)


def combine_kernel(want_ref, got_ref, grad_ref, out_ref, acc_ref):
    blocks, _, width = acc_ref.shape
    readers = want_ref.shape[0]
    for r in range(blocks):
        acc_ref[r] = grad_ref[:, r * width:(r + 1) * width]

    def body(step, carry):
        for j in range(8):
            reader = step * 8 + j
            for k in range(2):
                block = want_ref[reader, k]
                acc_ref[block] = acc_ref[block] + got_ref[reader * 2 + k].astype(F32)
        return carry

    lax.fori_loop(0, readers // 8, body, 0)
    for r in range(blocks):
        out_ref[:, r * width:(r + 1) * width] = acc_ref[r]


def per_device(embed, weight, cotangent, edge_masks, tile_rows, tile_owner, tile_sub):
    feats, nodes = embed.shape
    tiles, width, _ = edge_masks.shape
    blocks = nodes // width
    n_dom = lax.axis_size("dom")
    n_feat = lax.axis_size("feat")
    hidden = weight.shape[1]
    shape = jax.ShapeDtypeStruct
    swap = functools.partial(lax.all_to_all, axis_name="dom", split_axis=0, concat_axis=0, tiled=True)

    ask, slot = pl.pallas_call(
        slots_kernel,
        out_shape=(shape((n_dom, 128), jnp.int32), shape((1, tiles), jnp.int32)),
        in_specs=[VM, VM],
        out_specs=(VM, VM),
        compiler_params=params(4),
        name="slots",
    )(tile_owner.reshape(1, tiles), tile_sub.reshape(1, tiles))
    slot = slot.reshape(tiles)
    want = swap(ask)

    send = pl.pallas_call(
        select_kernel,
        out_shape=shape((2 * n_dom, feats, width), BF16),
        in_specs=[SM, VM],
        out_specs=VM,
        compiler_params=params(8),
        cost_estimate=cost(0, 2 * 2 * n_dom * feats * width * 2),
        name="select",
    )(want, embed)
    got = swap(send)

    full = lax.all_gather(jnp.concatenate([cotangent, weight], axis=1), "feat", axis=0, tiled=True)
    many = math.gcd(tiles, 12)
    mask, root = pl.pallas_call(
        masks_kernel,
        out_shape=(shape(edge_masks.shape, BF16), shape((blocks, 8, width), F32)),
        grid_spec=pltpu.PrefetchScalarGridSpec(
            num_scalar_prefetch=1,
            grid=(tiles // many,),
            in_specs=[pl.BlockSpec((many, width, width), lambda i, rows: (i, 0, 0))],
            out_specs=[
                pl.BlockSpec((many, width, width), lambda i, rows: (i, 0, 0)),
                pl.BlockSpec((blocks, 8, width), lambda i, rows: (0, 0, 0)),
            ],
            scratch_shapes=[pltpu.VMEM((blocks, 8, width), F32)],
        ),
        compiler_params=params(8),
        cost_estimate=cost(2 * tiles * 8 * width * width, 6 * tiles * width * width),
        name="masks",
    )(tile_rows, edge_masks)

    agg = pl.pallas_call(
        forward_kernel,
        out_shape=shape((feats, nodes), BF16),
        in_specs=[SM, SM, VM, VM, VM, VM],
        out_specs=VM,
        scratch_shapes=[pltpu.VMEM((blocks, feats, width), F32)],
        compiler_params=params(12),
        cost_estimate=cost(2 * tiles * feats * width * width, 2 * tiles * (feats + width) * width),
        name="forward",
    )(slot, tile_rows, got, mask, embed, root)

    agg_full = lax.all_gather(agg, "feat", axis=0, tiled=True)
    part = lax.axis_index("feat").astype(jnp.int32).reshape(1)
    out, grad, scaled, terms = pl.pallas_call(
        dense_kernel,
        out_shape=(
            shape((feats, nodes), BF16),
            shape((feats, nodes), F32),
            shape((blocks, feats, width), BF16),
            shape((feats, hidden), F32),
        ),
        in_specs=[SM, VM, VM, VM, VM, VM],
        out_specs=(VM, VM, VM, VM),
        scratch_shapes=[pltpu.VMEM((hidden, 2 * width), F32)],
        compiler_params=params(16),
        cost_estimate=cost(
            2 * hidden * (hidden + 2 * feats) * nodes, 2 * hidden * nodes * 3, hidden * nodes
        ),
        name="dense",
    )(part, agg_full, agg, full, weight, root)

    rows = swap(terms.reshape(n_dom, feats // n_dom, hidden))
    send_back = pl.pallas_call(
        backward_kernel,
        out_shape=shape((2 * n_dom, feats, width), BF16),
        in_specs=[SM, SM, VM, VM],
        out_specs=VM,
        compiler_params=params(12),
        cost_estimate=cost(2 * tiles * feats * width * width, 2 * tiles * (feats + width) * width),
        name="backward",
    )(slot, tile_rows, scaled, mask)
    got_back = swap(send_back)

    row = jnp.sum(rows, axis=0, keepdims=True) / math.sqrt(nodes * n_dom)
    weight_grad = swap(jnp.broadcast_to(row, (n_dom,) + row.shape[1:])).reshape(feats, hidden)

    embed_grad = pl.pallas_call(
        combine_kernel,
        out_shape=shape((feats, nodes), F32),
        in_specs=[SM, VM, VM],
        out_specs=VM,
        scratch_shapes=[pltpu.VMEM((blocks, feats, width), F32)],
        compiler_params=params(8),
        cost_estimate=cost(2 * n_dom * feats * width, 4 * n_dom * feats * width),
        name="combine",
    )(want, got_back, grad)
    return (out, embed_grad, weight_grad)


def solution(mesh):
    in_specs = (
        P("feat", "dom"),
        P("feat", None),
        P("feat", "dom"),
        P("dom", None, None),
        P("dom"),
        P("dom", None),
        P("dom"),
    )
    out_specs = (P("feat", "dom"), P("feat", "dom"), P("feat", None))
    return jax.shard_map(
        per_device, mesh=mesh, in_specs=in_specs, out_specs=out_specs, check_vma=False
    )
```

```python
import functools
import math

import jax
import jax.numpy as jnp
from jax import lax
from jax.experimental import pallas as pl
from jax.experimental.pallas import tpu as pltpu
from jax.sharding import Mesh, PartitionSpec as P

F32 = jnp.float32
BF16 = jnp.bfloat16
FEAT = "feat"
VM = pl.BlockSpec(memory_space=pltpu.VMEM)
SM = pl.BlockSpec(memory_space=pltpu.SMEM)


def params(mib):
    return pltpu.CompilerParams(vmem_limit_bytes=mib << 20)


def cost(flops, moved, exps=0):
    return pl.CostEstimate(flops=flops, bytes_accessed=moved, transcendentals=exps)


def slots_kernel(z_size, y_size, me_ref, owner_ref, across_ref, sub_ref, ask_ref, slot_ref):
    tiles = owner_ref.shape[0]

    def place(owner, before):
        y = owner % y_size
        z = (owner // y_size) % z_size
        x = owner // (y_size * z_size)
        return ((x * y_size + y) * z_size + z) * 2 + before

    down = lax.broadcasted_iota(jnp.int32, (tiles, tiles), 0)
    right = lax.broadcasted_iota(jnp.int32, (tiles, tiles), 1)
    same = owner_ref[...] == across_ref[...]
    before = jnp.sum((same & (right < down)).astype(jnp.int32), axis=1, keepdims=True)
    before_across = jnp.sum((same & (down < right)).astype(jnp.int32), axis=0, keepdims=True)
    slot_ref[...] = place(across_ref[...], before_across)
    lane = lax.broadcasted_iota(jnp.int32, (tiles, ask_ref.shape[1]), 1)
    asked = jnp.where(lane == place(owner_ref[...], before), sub_ref[...], 0)
    row = lax.broadcasted_iota(jnp.int32, ask_ref.shape, 0)
    ask_ref[...] = jnp.where(row == me_ref[0], jnp.sum(asked, axis=0, keepdims=True), 0)


def select_kernel(me_ref, want_ref, held_ref, send_ref):
    readers = want_ref.shape[0]
    owners = held_ref.shape[0]
    width = send_ref.shape[2]
    base = me_ref[0] * (2 * owners)

    def body(reader, carry):
        for z in range(owners):
            for k in range(2):
                start = pl.multiple_of(want_ref[reader, base + 2 * z + k] * width, width)
                send_ref[(reader * owners + z) * 2 + k] = held_ref[z, :, pl.ds(start, width)]
        return carry

    lax.fori_loop(0, readers, body, 0)


def masks_kernel(rows_ref, edge_ref, mask_ref, root_ref, degree_ref):
    step = pl.program_id(0)
    many = edge_ref.shape[0]

    @pl.when(step == 0)
    def _():
        degree_ref[...] = jnp.zeros_like(degree_ref)

    ones = jnp.ones((8, edge_ref.shape[2]), BF16)
    for j in range(many):
        mask = edge_ref[j].astype(F32).astype(BF16)
        mask_ref[j] = mask
        count = lax.dot_general(ones, mask, (((1,), (1,)), ((), ())), preferred_element_type=F32)
        row = rows_ref[step * many + j]
        degree_ref[row] = degree_ref[row] + count

    @pl.when(step == pl.num_programs(0) - 1)
    def _():
        root_ref[...] = 1.0 / jnp.sqrt(1.0 + degree_ref[...])


def forward_kernel(slot_ref, rows_ref, got_ref, mask_ref, own_ref, root_ref, agg_ref, acc_ref):
    tiles = mask_ref.shape[0]
    blocks, _, width = acc_ref.shape
    acc_ref[...] = jnp.zeros_like(acc_ref)
    group = 8

    def body(step, carry):
        terms = []
        for j in range(group):
            tile = step * group + j
            terms.append(
                lax.dot_general(
                    got_ref[slot_ref[tile]],
                    mask_ref[tile],
                    (((1,), (1,)), ((), ())),
                    preferred_element_type=F32,
                )
            )
        for j in range(group):
            row = rows_ref[step * group + j]
            acc_ref[row] = acc_ref[row] + terms[j]
        return carry

    lax.fori_loop(0, tiles // group, body, 0)
    for r in range(blocks):
        cols = slice(r * width, (r + 1) * width)
        agg_ref[:, cols] = (
            own_ref[:, cols].astype(F32) + acc_ref[r] * root_ref[r, 0:1, :]
        ).astype(BF16)


def dense_kernel(
    part_ref, agg_ref, aggown_ref, weight_ref, root_ref, *refs
):
    out_ref, grad_ref, scaled_ref, terms_ref, act_ref, full_ref = refs[-6:]
    parts = refs[:-6]
    nodes = agg_ref.shape[1]
    feats = weight_ref.shape[0]
    width = scaled_ref.shape[2]
    first = pl.multiple_of(part_ref[0] * feats, feats)
    for m, ref in enumerate(parts):
        start = pl.multiple_of((part_ref[0] ^ m) * feats, feats)
        full_ref[pl.ds(start, feats), :] = ref[...]
    chunk = 2 * width
    terms = jnp.zeros(terms_ref.shape, F32)
    for c in range(nodes // chunk):
        cols = slice(c * chunk, (c + 1) * chunk)
        pre = lax.dot_general(
            full_ref[:, nodes:], agg_ref[:, cols], (((0,), (0,)), ((), ())), preferred_element_type=F32
        )
        gate = jax.nn.sigmoid(pre)
        act_ref[...] = pre * gate
        out_ref[:, cols] = act_ref[pl.ds(first, feats), :].astype(BF16)
        grad_pre = (full_ref[:, cols].astype(F32) * gate * (1.0 + pre * (1.0 - gate))).astype(BF16)
        grad = jnp.dot(weight_ref[...], grad_pre, preferred_element_type=F32)
        grad_ref[:, cols] = grad
        terms = terms + lax.dot_general(
            aggown_ref[:, cols], grad_pre, (((1,), (1,)), ((), ())), preferred_element_type=F32
        )
        for k in range(2):
            r = 2 * c + k
            scaled_ref[r] = (grad[:, k * width:(k + 1) * width] * root_ref[r, 0:1, :]).astype(BF16)
    terms_ref[...] = terms


def backward_kernel(slot_ref, rows_ref, scaled_ref, mask_ref, send_ref):
    tiles = mask_ref.shape[0]
    group = 8
    send_ref[...] = jnp.zeros_like(send_ref)

    def body(step, carry):
        for j in range(group):
            tile = step * group + j
            send_ref[slot_ref[tile]] = jnp.dot(
                scaled_ref[rows_ref[tile]], mask_ref[tile], preferred_element_type=F32
            ).astype(BF16)
        return carry

    lax.fori_loop(0, tiles // group, body, 0)


def gather_kernel(me_ref, want_ref, got_ref, sum_ref, acc_ref):
    owners, blocks, _, width = acc_ref.shape
    readers = want_ref.shape[0]
    base = me_ref[0] * (2 * owners)
    acc_ref[...] = jnp.zeros_like(acc_ref)

    def body(reader, carry):
        for z in range(owners):
            for k in range(2):
                block = want_ref[reader, base + 2 * z + k]
                acc_ref[z, block] = acc_ref[z, block] + got_ref[(reader * owners + z) * 2 + k].astype(F32)
        return carry

    lax.fori_loop(0, readers, body, 0)
    for z in range(owners):
        for r in range(blocks):
            sum_ref[z, :, r * width:(r + 1) * width] = acc_ref[z, r].astype(BF16)


def combine_kernel(got_ref, grad_ref, out_ref):
    total = grad_ref[...]
    for z in range(got_ref.shape[0]):
        total = total + got_ref[z].astype(F32)
    out_ref[...] = total


def pairwise(value, axes):
    for name, size in axes:
        bit = 1
        while bit < size:
            value = value + lax.ppermute(value, name, [(i, i ^ bit) for i in range(size)])
            bit *= 2
    return value


def per_device(embed, weight, cotangent, edge_masks, tile_rows, tile_owner, tile_sub):
    feats, nodes = embed.shape
    tiles, width, _ = edge_masks.shape
    blocks = nodes // width
    n_x, n_z, n_y = (lax.axis_size(name) for name in ("x", "z", "y_lo"))
    plane = ("x", "y_lo")
    peers = n_x * n_y
    slots = peers * n_z * 2
    hidden = weight.shape[1]
    shape = jax.ShapeDtypeStruct
    swap = functools.partial(lax.all_to_all, split_axis=0, concat_axis=0, tiled=True)

    held = swap(jnp.broadcast_to(embed[None], (n_z, feats, nodes)), "z")
    me = (lax.axis_index("x") * n_y + lax.axis_index("y_lo")).astype(jnp.int32).reshape(1)
    ask, slot = pl.pallas_call(
        functools.partial(slots_kernel, n_z, n_y),
        out_shape=(shape((peers, slots), jnp.int32), shape((1, tiles), jnp.int32)),
        in_specs=[SM, VM, VM, VM],
        out_specs=(VM, VM),
        compiler_params=params(4),
        name="slots",
    )(me, tile_owner, tile_owner.reshape(1, tiles), tile_sub.reshape(tiles, 1))
    slot = slot.reshape(tiles)
    want = pairwise(ask, (("y_lo", n_y), ("x", n_x)))

    mine = jnp.concatenate([cotangent, weight], axis=1)
    n_feat = hidden // feats
    parts = [mine] + [
        lax.ppermute(mine, FEAT, [(i, i ^ m) for i in range(n_feat)]) for m in range(1, n_feat)
    ]
    many = math.gcd(tiles, 12)
    mask, root = pl.pallas_call(
        masks_kernel,
        out_shape=(shape(edge_masks.shape, BF16), shape((blocks, 8, width), F32)),
        grid_spec=pltpu.PrefetchScalarGridSpec(
            num_scalar_prefetch=1,
            grid=(tiles // many,),
            in_specs=[pl.BlockSpec((many, width, width), lambda i, rows: (i, 0, 0))],
            out_specs=[
                pl.BlockSpec((many, width, width), lambda i, rows: (i, 0, 0)),
                pl.BlockSpec((blocks, 8, width), lambda i, rows: (0, 0, 0)),
            ],
            scratch_shapes=[pltpu.VMEM((blocks, 8, width), F32)],
        ),
        compiler_params=params(8),
        cost_estimate=cost(2 * tiles * 8 * width * width, 6 * tiles * width * width),
        name="masks",
    )(tile_rows, edge_masks)

    part = lax.axis_index(FEAT).astype(jnp.int32).reshape(1)
    held, parts, part, mask, root = lax.optimization_barrier((held, parts, part, mask, root))
    send = pl.pallas_call(
        select_kernel,
        out_shape=shape((slots, feats, width), BF16),
        in_specs=[SM, SM, VM],
        out_specs=VM,
        compiler_params=params(8),
        cost_estimate=cost(0, 2 * slots * feats * width * 2),
        name="select",
    )(me, want, held)
    got = swap(send, plane)

    agg = pl.pallas_call(
        forward_kernel,
        out_shape=shape((feats, nodes), BF16),
        in_specs=[SM, SM, VM, VM, VM, VM],
        out_specs=VM,
        scratch_shapes=[pltpu.VMEM((blocks, feats, width), F32)],
        compiler_params=params(12),
        cost_estimate=cost(2 * tiles * feats * width * width, 2 * tiles * (feats + width) * width),
        name="forward",
    )(slot, tile_rows, got, mask, embed, root)

    agg_full = lax.all_gather(agg, FEAT, axis=0, tiled=True)
    out, grad, scaled, terms = pl.pallas_call(
        dense_kernel,
        out_shape=(
            shape((feats, nodes), BF16),
            shape((feats, nodes), F32),
            shape((blocks, feats, width), BF16),
            shape((feats, hidden), F32),
        ),
        in_specs=[SM] + [VM] * (4 + n_feat),
        out_specs=(VM, VM, VM, VM),
        scratch_shapes=[
            pltpu.VMEM((hidden, 2 * width), F32),
            pltpu.VMEM((hidden, nodes + hidden), BF16),
        ],
        compiler_params=params(16),
        cost_estimate=cost(
            2 * hidden * (hidden + 2 * feats) * nodes, 2 * hidden * nodes * 3, hidden * nodes
        ),
        name="dense",
    )(part, agg_full, agg, weight, root, *parts)

    send_back = pl.pallas_call(
        backward_kernel,
        out_shape=shape((slots, feats, width), BF16),
        in_specs=[SM, SM, VM, VM],
        out_specs=VM,
        compiler_params=params(12),
        cost_estimate=cost(2 * tiles * feats * width * width, 2 * tiles * (feats + width) * width),
        name="backward",
    )(slot, tile_rows, scaled, mask)
    got_back = swap(send_back, plane)

    terms = pairwise(terms, (("z", n_z),))
    got_back, terms = lax.optimization_barrier((got_back, terms))
    terms = pairwise(terms, (("y_lo", n_y), ("x", n_x)))
    weight_grad = terms / math.sqrt(nodes * n_x * n_z * n_y)

    sums = pl.pallas_call(
        gather_kernel,
        out_shape=shape((n_z, feats, nodes), BF16),
        in_specs=[SM, SM, VM],
        out_specs=VM,
        scratch_shapes=[pltpu.VMEM((n_z, blocks, feats, width), F32)],
        compiler_params=params(12),
        cost_estimate=cost(slots * feats * width, 4 * slots * feats * width),
        name="gather",
    )(me, want, got_back)
    got_sums = swap(sums, "z")
    embed_grad = pl.pallas_call(
        combine_kernel,
        out_shape=shape((feats, nodes), F32),
        in_specs=[VM, VM],
        out_specs=VM,
        compiler_params=params(8),
        cost_estimate=cost(n_z * feats * nodes, 2 * n_z * feats * nodes),
        name="combine",
    )(got_sums, grad)
    return (out, embed_grad, weight_grad)


def solution(mesh):
    n_dom, n_feat = mesh.devices.shape
    wide = Mesh(mesh.devices.reshape(n_dom // 16, 8, 2, n_feat), ("x", "z", "y_lo", FEAT))
    dom = ("x", "z", "y_lo")
    in_specs = (
        P(FEAT, dom),
        P(FEAT, None),
        P(FEAT, dom),
        P(dom, None, None),
        P(dom),
        P(dom, None),
        P(dom),
    )
    out_specs = (P(FEAT, dom), P(FEAT, dom), P(FEAT, None))
    return jax.shard_map(
        per_device, mesh=wide, in_specs=in_specs, out_specs=out_specs, check_vma=False
    )
```

```python
import functools
import math

import jax
import jax.numpy as jnp
from jax import lax
from jax.experimental import pallas as pl
from jax.experimental.pallas import tpu as pltpu
from jax.sharding import Mesh, PartitionSpec as P

F32 = jnp.float32
BF16 = jnp.bfloat16
FEAT = "feat"
VM = pl.BlockSpec(memory_space=pltpu.VMEM)
SM = pl.BlockSpec(memory_space=pltpu.SMEM)


def params(mib):
    return pltpu.CompilerParams(vmem_limit_bytes=mib << 20)


def cost(flops, moved, exps=0):
    return pl.CostEstimate(flops=flops, bytes_accessed=moved, transcendentals=exps)


def slots_kernel(z_size, y_size, me_ref, owner_ref, across_ref, sub_ref, ask_ref, slot_ref):
    tiles = owner_ref.shape[0]

    def place(owner, before):
        y = owner % y_size
        z = (owner // y_size) % z_size
        x = owner // (y_size * z_size)
        return ((x * y_size + y) * z_size + z) * 2 + before

    down = lax.broadcasted_iota(jnp.int32, (tiles, tiles), 0)
    right = lax.broadcasted_iota(jnp.int32, (tiles, tiles), 1)
    same = owner_ref[...] == across_ref[...]
    before = jnp.sum((same & (right < down)).astype(jnp.int32), axis=1, keepdims=True)
    before_across = jnp.sum((same & (down < right)).astype(jnp.int32), axis=0, keepdims=True)
    slot_ref[...] = place(across_ref[...], before_across)
    lane = lax.broadcasted_iota(jnp.int32, (tiles, ask_ref.shape[1]), 1)
    asked = jnp.where(lane == place(owner_ref[...], before), sub_ref[...], 0)
    row = lax.broadcasted_iota(jnp.int32, ask_ref.shape, 0)
    ask_ref[...] = jnp.where(row == me_ref[0], jnp.sum(asked, axis=0, keepdims=True), 0)


def select_kernel(me_ref, want_ref, held_ref, send_ref):
    readers = want_ref.shape[0]
    owners = held_ref.shape[0]
    width = send_ref.shape[2]
    base = me_ref[0] * (2 * owners)

    def body(reader, carry):
        for z in range(owners):
            for k in range(2):
                start = pl.multiple_of(want_ref[reader, base + 2 * z + k] * width, width)
                send_ref[(reader * owners + z) * 2 + k] = held_ref[z, :, pl.ds(start, width)]
        return carry

    lax.fori_loop(0, readers, body, 0)


def masks_kernel(rows_ref, edge_ref, mask_ref, root_ref, degree_ref):
    step = pl.program_id(0)
    many = edge_ref.shape[0]

    @pl.when(step == 0)
    def _():
        degree_ref[...] = jnp.zeros_like(degree_ref)

    ones = jnp.ones((8, edge_ref.shape[2]), BF16)
    for j in range(many):
        mask = edge_ref[j].astype(F32).astype(BF16)
        mask_ref[j] = mask
        count = lax.dot_general(ones, mask, (((1,), (1,)), ((), ())), preferred_element_type=F32)
        row = rows_ref[step * many + j]
        degree_ref[row] = degree_ref[row] + count

    @pl.when(step == pl.num_programs(0) - 1)
    def _():
        root_ref[...] = 1.0 / jnp.sqrt(1.0 + degree_ref[...])


def forward_kernel(slot_ref, rows_ref, got_ref, mask_ref, own_ref, root_ref, agg_ref, acc_ref):
    tiles = mask_ref.shape[0]
    blocks, _, width = acc_ref.shape
    acc_ref[...] = jnp.zeros_like(acc_ref)
    group = 8

    def body(step, carry):
        terms = []
        for j in range(group):
            tile = step * group + j
            terms.append(
                lax.dot_general(
                    got_ref[slot_ref[tile]],
                    mask_ref[tile],
                    (((1,), (1,)), ((), ())),
                    preferred_element_type=F32,
                )
            )
        for j in range(group):
            row = rows_ref[step * group + j]
            acc_ref[row] = acc_ref[row] + terms[j]
        return carry

    lax.fori_loop(0, tiles // group, body, 0)
    for r in range(blocks):
        cols = slice(r * width, (r + 1) * width)
        agg_ref[:, cols] = (
            own_ref[:, cols].astype(F32) + acc_ref[r] * root_ref[r, 0:1, :]
        ).astype(BF16)


def dense_kernel(
    part_ref, agg_ref, aggown_ref, weight_ref, root_ref, *refs
):
    out_ref, grad_ref, scaled_ref, terms_ref, act_ref, full_ref = refs[-6:]
    parts = refs[:-6]
    nodes = agg_ref.shape[1]
    feats = weight_ref.shape[0]
    width = scaled_ref.shape[2]
    first = pl.multiple_of(part_ref[0] * feats, feats)
    for m, ref in enumerate(parts):
        start = pl.multiple_of((part_ref[0] ^ m) * feats, feats)
        full_ref[pl.ds(start, feats), :] = ref[...]
    chunk = 2 * width
    terms = jnp.zeros(terms_ref.shape, F32)
    for c in range(nodes // chunk):
        cols = slice(c * chunk, (c + 1) * chunk)
        pre = lax.dot_general(
            full_ref[:, nodes:], agg_ref[:, cols], (((0,), (0,)), ((), ())), preferred_element_type=F32
        )
        gate = jax.nn.sigmoid(pre)
        act_ref[...] = pre * gate
        out_ref[:, cols] = act_ref[pl.ds(first, feats), :].astype(BF16)
        grad_pre = (full_ref[:, cols].astype(F32) * gate * (1.0 + pre * (1.0 - gate))).astype(BF16)
        grad = jnp.dot(weight_ref[...], grad_pre, preferred_element_type=F32)
        grad_ref[:, cols] = grad
        terms = terms + lax.dot_general(
            aggown_ref[:, cols], grad_pre, (((1,), (1,)), ((), ())), preferred_element_type=F32
        )
        for k in range(2):
            r = 2 * c + k
            scaled_ref[r] = (grad[:, k * width:(k + 1) * width] * root_ref[r, 0:1, :]).astype(BF16)
    terms_ref[...] = terms


def backward_kernel(slot_ref, rows_ref, scaled_ref, mask_ref, terms_ref, send_ref):
    tiles = mask_ref.shape[0]
    feats, hidden = terms_ref.shape
    width = send_ref.shape[2]
    end = send_ref.shape[1] - feats * hidden // width
    per_peer = end // feats
    group = 8
    send_ref[:, :end, :] = jnp.zeros((send_ref.shape[0], end, width), BF16)

    def body(step, carry):
        for j in range(group):
            tile = step * group + j
            slot = slot_ref[tile]
            start = pl.multiple_of((slot % per_peer) * feats, feats)
            send_ref[slot // per_peer, pl.ds(start, feats), :] = jnp.dot(
                scaled_ref[rows_ref[tile]], mask_ref[tile], preferred_element_type=F32
            ).astype(BF16)
        return carry

    lax.fori_loop(0, tiles // group, body, 0)
    for h in range(hidden // width):
        part = terms_ref[:, h * width:(h + 1) * width].astype(BF16)
        for p in range(send_ref.shape[0]):
            send_ref[p, end + h * feats:end + (h + 1) * feats, :] = part


def gather_kernel(me_ref, want_ref, got_ref, up_ref, down_ref, *refs):
    acc_ref = refs[-1]
    sums = refs[:-1]
    owners, blocks, feats, width = acc_ref.shape
    readers = want_ref.shape[0]
    base = me_ref[0] * (2 * owners)
    acc_ref[...] = jnp.zeros_like(acc_ref)

    def body(reader, carry):
        for z in range(owners):
            for k in range(2):
                block = want_ref[reader, base + 2 * z + k]
                start = (2 * z + k) * feats
                acc_ref[z, block] = acc_ref[z, block] + got_ref[reader, start:start + feats, :].astype(F32)
        return carry

    lax.fori_loop(0, readers, body, 0)
    end = 2 * owners * feats
    low = up_ref.shape[0] - feats
    for h in range((got_ref.shape[1] - end) // low):
        rows = slice(end + h * low, end + (h + 1) * low)
        terms = got_ref[0, rows, :].astype(F32)
        for q in range(1, readers):
            terms = terms + got_ref[q, rows, :].astype(F32)
        up_ref[feats:, h * width:(h + 1) * width] = terms.astype(BF16)
        down_ref[feats:, h * width:(h + 1) * width] = terms.astype(BF16)
    half = owners // 2
    for d in range(owners):
        ref = up_ref if d == half else down_ref if d == half + 1 else sums[d - 2 * (d > half)]
        z = (me_ref[1] + d) % owners
        for r in range(blocks):
            ref[:feats, r * width:(r + 1) * width] = acc_ref[z, r].astype(ref.dtype)


def hop_kernel(*refs):
    many = len(refs) // 3
    for got_ref, sum_ref, on_ref in zip(refs[:many], refs[many:2 * many], refs[2 * many:]):
        feats = sum_ref.shape[0]
        on_ref[:feats, :] = (got_ref[:feats, :].astype(F32) + sum_ref[...]).astype(BF16)
        on_ref[feats:, :] = got_ref[feats:, :]


def combine_kernel(scale, me_ref, grad_ref, own_ref, *refs):
    out_ref, weight_ref, terms_ref = refs[-3:]
    places = refs[:-3]
    planes = len(places)
    feats, hidden = weight_ref.shape
    low, nodes = terms_ref.shape[1:]
    half = planes // 2
    out_ref[...] = grad_ref[...] + own_ref[...] + (
        places[planes - half][:feats, :].astype(F32) + places[half - 1][:feats, :].astype(F32)
    )
    for d, ref in enumerate(places):
        terms_ref[(me_ref[1] + d) % planes] = ref[feats:, :].astype(F32)
    total = terms_ref[0]
    for z in range(1, planes):
        total = total + terms_ref[z]
    total = total * scale
    lanes = 128
    per = feats // low
    for h in range(hidden // lanes):
        for g in range(per):
            start = (h * per + g) * lanes
            weight_ref[g * low:(g + 1) * low, h * lanes:(h + 1) * lanes] = total[:, start:start + lanes]


def pairwise(value, axes):
    for name, size in axes:
        bit = 1
        while bit < size:
            value = value + lax.ppermute(value, name, [(i, i ^ bit) for i in range(size)])
            bit *= 2
    return value


def per_device(embed, weight, cotangent, edge_masks, tile_rows, tile_owner, tile_sub):
    feats, nodes = embed.shape
    tiles, width, _ = edge_masks.shape
    blocks = nodes // width
    n_x, n_z, n_y = (lax.axis_size(name) for name in ("x", "z", "y_lo"))
    plane = ("x", "y_lo")
    peers = n_x * n_y
    slots = peers * n_z * 2
    hidden = weight.shape[1]
    shape = jax.ShapeDtypeStruct
    swap = functools.partial(lax.all_to_all, split_axis=0, concat_axis=0, tiled=True)

    held = swap(jnp.broadcast_to(embed[None], (n_z, feats, nodes)), "z")
    me = jnp.stack([lax.axis_index("x") * n_y + lax.axis_index("y_lo"), lax.axis_index("z")])
    me = me.astype(jnp.int32)
    ask, slot = pl.pallas_call(
        functools.partial(slots_kernel, n_z, n_y),
        out_shape=(shape((peers, slots), jnp.int32), shape((1, tiles), jnp.int32)),
        in_specs=[SM, VM, VM, VM],
        out_specs=(VM, VM),
        compiler_params=params(4),
        name="slots",
    )(me, tile_owner, tile_owner.reshape(1, tiles), tile_sub.reshape(tiles, 1))
    slot = slot.reshape(tiles)
    want = pairwise(ask, (("y_lo", n_y), ("x", n_x)))

    mine = jnp.concatenate([cotangent, weight], axis=1)
    n_feat = hidden // feats
    parts = [mine] + [
        lax.ppermute(mine, FEAT, [(i, i ^ m) for i in range(n_feat)]) for m in range(1, n_feat)
    ]
    many = math.gcd(tiles, 12)
    mask, root = pl.pallas_call(
        masks_kernel,
        out_shape=(shape(edge_masks.shape, BF16), shape((blocks, 8, width), F32)),
        grid_spec=pltpu.PrefetchScalarGridSpec(
            num_scalar_prefetch=1,
            grid=(tiles // many,),
            in_specs=[pl.BlockSpec((many, width, width), lambda i, rows: (i, 0, 0))],
            out_specs=[
                pl.BlockSpec((many, width, width), lambda i, rows: (i, 0, 0)),
                pl.BlockSpec((blocks, 8, width), lambda i, rows: (0, 0, 0)),
            ],
            scratch_shapes=[pltpu.VMEM((blocks, 8, width), F32)],
        ),
        compiler_params=params(8),
        cost_estimate=cost(2 * tiles * 8 * width * width, 6 * tiles * width * width),
        name="masks",
    )(tile_rows, edge_masks)

    part = lax.axis_index(FEAT).astype(jnp.int32).reshape(1)
    held, parts, part, mask, root = lax.optimization_barrier((held, parts, part, mask, root))
    send = pl.pallas_call(
        select_kernel,
        out_shape=shape((slots, feats, width), BF16),
        in_specs=[SM, SM, VM],
        out_specs=VM,
        compiler_params=params(8),
        cost_estimate=cost(0, 2 * slots * feats * width * 2),
        name="select",
    )(me, want, held)
    got = swap(send, plane)

    agg = pl.pallas_call(
        forward_kernel,
        out_shape=shape((feats, nodes), BF16),
        in_specs=[SM, SM, VM, VM, VM, VM],
        out_specs=VM,
        scratch_shapes=[pltpu.VMEM((blocks, feats, width), F32)],
        compiler_params=params(12),
        cost_estimate=cost(2 * tiles * feats * width * width, 2 * tiles * (feats + width) * width),
        name="forward",
    )(slot, tile_rows, got, mask, embed, root)

    agg_full = lax.all_gather(agg, FEAT, axis=0, tiled=True)
    out, grad, scaled, terms = pl.pallas_call(
        dense_kernel,
        out_shape=(
            shape((feats, nodes), BF16),
            shape((feats, nodes), F32),
            shape((blocks, feats, width), BF16),
            shape((feats, hidden), F32),
        ),
        in_specs=[SM] + [VM] * (4 + n_feat),
        out_specs=(VM, VM, VM, VM),
        scratch_shapes=[
            pltpu.VMEM((hidden, 2 * width), F32),
            pltpu.VMEM((hidden, nodes + hidden), BF16),
        ],
        compiler_params=params(16),
        cost_estimate=cost(
            2 * hidden * (hidden + 2 * feats) * nodes, 2 * hidden * nodes * 3, hidden * nodes
        ),
        name="dense",
    )(part, agg_full, agg, weight, root, *parts)

    extra = feats * hidden // width
    send_back = pl.pallas_call(
        backward_kernel,
        out_shape=shape((peers, 2 * n_z * feats + extra, width), BF16),
        in_specs=[SM, SM, VM, VM, VM],
        out_specs=VM,
        compiler_params=params(12),
        cost_estimate=cost(2 * tiles * feats * width * width, 2 * tiles * (feats + width) * width),
        name="backward",
    )(slot, tile_rows, scaled, mask, terms)
    got_back = swap(send_back, plane)

    half = n_z // 2
    low = feats * hidden // nodes
    message = shape((feats + low, nodes), BF16)
    plain = shape((feats, nodes), F32)
    up, down, *sums = pl.pallas_call(
        gather_kernel,
        out_shape=[message, message] + [plain] * (n_z - 2),
        in_specs=[SM, SM, VM],
        out_specs=[VM] * n_z,
        scratch_shapes=[pltpu.VMEM((n_z, blocks, feats, width), F32)],
        compiler_params=params(16),
        cost_estimate=cost(slots * feats * width, 4 * slots * feats * width),
        name="gather",
    )(me, want, got_back)
    sums[half:half] = [None, None]
    onward = [(i, (i + 1) % n_z) for i in range(n_z)]
    back = [(i, (i - 1) % n_z) for i in range(n_z)]
    places = [up] * n_z
    for hop in range(half):
        up = lax.ppermute(up, "z", onward)
        places[n_z - 1 - hop] = up
        if hop == half - 1:
            break
        down = lax.ppermute(down, "z", back)
        places[hop + 1] = down
        if hop < half - 2:
            up, down = pl.pallas_call(
                hop_kernel,
                out_shape=(message, message),
                in_specs=[VM] * 4,
                out_specs=(VM, VM),
                compiler_params=params(4),
                name="hop",
            )(up, down, sums[half - 1 - hop], sums[half + 2 + hop])
        else:
            up = pl.pallas_call(
                hop_kernel,
                out_shape=message,
                in_specs=[VM] * 2,
                out_specs=VM,
                compiler_params=params(4),
                name="hop",
            )(up, sums[half - 1 - hop])
    embed_grad, weight_grad = pl.pallas_call(
        functools.partial(combine_kernel, 1.0 / math.sqrt(nodes * n_x * n_z * n_y)),
        out_shape=(plain, shape((feats, hidden), F32)),
        in_specs=[SM] + [VM] * (2 + n_z),
        out_specs=(VM, VM),
        scratch_shapes=[pltpu.VMEM((n_z, low, nodes), F32)],
        compiler_params=params(8),
        cost_estimate=cost(3 * feats * nodes, 16 * feats * nodes),
        name="combine",
    )(me, grad, sums[0], *places)
    return (out, embed_grad, weight_grad)


def solution(mesh):
    n_dom, n_feat = mesh.devices.shape
    wide = Mesh(mesh.devices.reshape(n_dom // 16, 8, 2, n_feat), ("x", "z", "y_lo", FEAT))
    dom = ("x", "z", "y_lo")
    in_specs = (
        P(FEAT, dom),
        P(FEAT, None),
        P(FEAT, dom),
        P(dom, None, None),
        P(dom),
        P(dom, None),
        P(dom),
    )
    out_specs = (P(FEAT, dom), P(FEAT, dom), P(FEAT, None))
    return jax.shard_map(
        per_device, mesh=wide, in_specs=in_specs, out_specs=out_specs, check_vma=False
    )
```

```python
import functools
import math

import jax
import jax.numpy as jnp
from jax import lax
from jax.experimental import pallas as pl
from jax.experimental.pallas import tpu as pltpu
from jax.sharding import Mesh, PartitionSpec as P

F32 = jnp.float32
BF16 = jnp.bfloat16
FEAT = "feat"
VM = pl.BlockSpec(memory_space=pltpu.VMEM)
SM = pl.BlockSpec(memory_space=pltpu.SMEM)


def params(mib):
    return pltpu.CompilerParams(vmem_limit_bytes=mib << 20)


def cost(flops, moved, exps=0):
    return pl.CostEstimate(flops=flops, bytes_accessed=moved, transcendentals=exps)


def slots_kernel(z_size, y_size, me_ref, owner_ref, across_ref, sub_ref, ask_ref, slot_ref):
    tiles = owner_ref.shape[0]

    def place(owner, before):
        y = owner % y_size
        z = (owner // y_size) % z_size
        x = owner // (y_size * z_size)
        return ((x * y_size + y) * z_size + z) * 2 + before

    down = lax.broadcasted_iota(jnp.int32, (tiles, tiles), 0)
    right = lax.broadcasted_iota(jnp.int32, (tiles, tiles), 1)
    same = owner_ref[...] == across_ref[...]
    before = jnp.sum((same & (right < down)).astype(jnp.int32), axis=1, keepdims=True)
    before_across = jnp.sum((same & (down < right)).astype(jnp.int32), axis=0, keepdims=True)
    slot_ref[...] = place(across_ref[...], before_across)
    lane = lax.broadcasted_iota(jnp.int32, (tiles, ask_ref.shape[1]), 1)
    asked = jnp.where(lane == place(owner_ref[...], before), sub_ref[...], 0)
    row = lax.broadcasted_iota(jnp.int32, ask_ref.shape, 0)
    ask_ref[...] = jnp.where(row == me_ref[0], jnp.sum(asked, axis=0, keepdims=True), 0)


def select_kernel(me_ref, want_ref, held_ref, send_ref):
    readers = want_ref.shape[0]
    owners = held_ref.shape[0]
    width = send_ref.shape[2]
    base = me_ref[0] * (2 * owners)

    def body(reader, carry):
        for z in range(owners):
            for k in range(2):
                start = pl.multiple_of(want_ref[reader, base + 2 * z + k] * width, width)
                send_ref[(reader * owners + z) * 2 + k] = held_ref[z, :, pl.ds(start, width)]
        return carry

    lax.fori_loop(0, readers, body, 0)


def forward_kernel(slot_ref, rows_ref, got_ref, edge_ref, own_ref, agg_ref, root_ref, acc_ref):
    tiles, width, _ = edge_ref.shape
    blocks = acc_ref.shape[0]
    feats = got_ref.shape[1]
    acc_ref[...] = jnp.zeros_like(acc_ref)
    group = 8
    ones = jnp.ones((16, width), BF16)

    def body(step, carry):
        terms = []
        for j in range(group):
            tile = step * group + j
            mask = edge_ref[tile].astype(F32).astype(BF16)
            left = jnp.concatenate([got_ref[slot_ref[tile]], ones], axis=0)
            terms.append(
                lax.dot_general(left, mask, (((1,), (1,)), ((), ())), preferred_element_type=F32)
            )
        for j in range(group):
            row = rows_ref[step * group + j]
            acc_ref[row] = acc_ref[row] + terms[j][:feats + 8]
        return carry

    lax.fori_loop(0, tiles // group, body, 0)
    for r in range(blocks):
        cols = slice(r * width, (r + 1) * width)
        root = 1.0 / jnp.sqrt(1.0 + acc_ref[r, feats:feats + 8, :])
        root_ref[r] = root
        agg_ref[:, cols] = (
            own_ref[:, cols].astype(F32) + acc_ref[r, :feats, :] * root[0:1, :]
        ).astype(BF16)


def order_kernel(part_ref, *refs):
    full_ref = refs[-1]
    for m, ref in enumerate(refs[:-1]):
        feats = ref.shape[0]
        start = pl.multiple_of((part_ref[0] ^ m) * feats, feats)
        full_ref[pl.ds(start, feats), :] = ref[...]


def dense_kernel(
    part_ref, agg_ref, aggown_ref, full_ref, weight_ref, root_ref,
    out_ref, grad_ref, scaled_ref, terms_ref, act_ref,
):
    nodes = agg_ref.shape[1]
    feats = weight_ref.shape[0]
    width = scaled_ref.shape[2]
    first = pl.multiple_of(part_ref[0] * feats, feats)
    chunk = 2 * width
    terms = jnp.zeros(terms_ref.shape, F32)
    for c in range(nodes // chunk):
        cols = slice(c * chunk, (c + 1) * chunk)
        pre = lax.dot_general(
            full_ref[:, nodes:], agg_ref[:, cols], (((0,), (0,)), ((), ())), preferred_element_type=F32
        )
        gate = jax.nn.sigmoid(pre)
        act_ref[...] = pre * gate
        out_ref[:, cols] = act_ref[pl.ds(first, feats), :].astype(BF16)
        grad_pre = (full_ref[:, cols].astype(F32) * gate * (1.0 + pre * (1.0 - gate))).astype(BF16)
        grad = jnp.dot(weight_ref[...], grad_pre, preferred_element_type=F32)
        grad_ref[:, cols] = grad
        terms = terms + lax.dot_general(
            aggown_ref[:, cols], grad_pre, (((1,), (1,)), ((), ())), preferred_element_type=F32
        )
        for k in range(2):
            r = 2 * c + k
            scaled_ref[r] = (grad[:, k * width:(k + 1) * width] * root_ref[r, 0:1, :]).astype(BF16)
    terms_ref[...] = terms


def backward_kernel(slot_ref, rows_ref, scaled_ref, edge_ref, terms_ref, send_ref):
    tiles = edge_ref.shape[0]
    feats, hidden = terms_ref.shape
    width = send_ref.shape[2]
    end = send_ref.shape[1] - feats * hidden // width
    per_peer = end // feats
    group = 8
    send_ref[:, :end, :] = jnp.zeros((send_ref.shape[0], end, width), BF16)

    def body(step, carry):
        for j in range(group):
            tile = step * group + j
            slot = slot_ref[tile]
            start = pl.multiple_of((slot % per_peer) * feats, feats)
            send_ref[slot // per_peer, pl.ds(start, feats), :] = jnp.dot(
                scaled_ref[rows_ref[tile]],
                edge_ref[tile].astype(F32).astype(BF16),
                preferred_element_type=F32,
            ).astype(BF16)
        return carry

    lax.fori_loop(0, tiles // group, body, 0)
    for h in range(hidden // width):
        part = terms_ref[:, h * width:(h + 1) * width].astype(BF16)
        for p in range(send_ref.shape[0]):
            send_ref[p, end + h * feats:end + (h + 1) * feats, :] = part


def add_up(distances, me_ref, want_ref, got_ref, acc_ref, owners):
    _, blocks, feats, width = acc_ref.shape
    readers = want_ref.shape[0]
    base = me_ref[0] * (2 * owners)

    def body(reader, carry):
        for i, d in enumerate(distances):
            z = (me_ref[1] + d) % owners
            for k in range(2):
                block = want_ref[reader, base + 2 * z + k]
                start = pl.multiple_of((2 * z + k) * feats, feats)
                acc_ref[i, block] = acc_ref[i, block] + got_ref[reader, pl.ds(start, feats), :].astype(F32)
        return carry

    lax.fori_loop(0, readers, body, 0)


def start_kernel(owners, me_ref, want_ref, got_ref, up_ref, down_ref, acc_ref):
    _, blocks, feats, width = acc_ref.shape
    half = owners // 2
    acc_ref[...] = jnp.zeros_like(acc_ref)
    add_up((half, half + 1), me_ref, want_ref, got_ref, acc_ref, owners)
    end = 2 * owners * feats
    low = up_ref.shape[0] - feats
    for h in range((got_ref.shape[1] - end) // low):
        rows = slice(end + h * low, end + (h + 1) * low)
        terms = got_ref[0, rows, :].astype(F32)
        for q in range(1, got_ref.shape[0]):
            terms = terms + got_ref[q, rows, :].astype(F32)
        up_ref[feats:, h * width:(h + 1) * width] = terms.astype(BF16)
        down_ref[feats:, h * width:(h + 1) * width] = terms.astype(BF16)
    for i, ref in enumerate((up_ref, down_ref)):
        for r in range(blocks):
            ref[:feats, r * width:(r + 1) * width] = acc_ref[i, r].astype(BF16)


def gather_kernel(owners, me_ref, want_ref, got_ref, grad_ref, *refs):
    acc_ref = refs[-1]
    _, blocks, feats, width = acc_ref.shape
    half = owners // 2
    acc_ref[...] = jnp.zeros_like(acc_ref)
    for r in range(blocks):
        acc_ref[0, r] = grad_ref[:, r * width:(r + 1) * width]
    distances = [d for d in range(owners) if d not in (half, half + 1)]
    add_up(distances, me_ref, want_ref, got_ref, acc_ref, owners)
    for i, ref in enumerate(refs[:-1]):
        for r in range(blocks):
            ref[:, r * width:(r + 1) * width] = acc_ref[i, r]


def hop_kernel(*refs):
    many = len(refs) // 3
    for got_ref, sum_ref, on_ref in zip(refs[:many], refs[many:2 * many], refs[2 * many:]):
        feats = sum_ref.shape[0]
        on_ref[:feats, :] = (got_ref[:feats, :].astype(F32) + sum_ref[...]).astype(BF16)
        on_ref[feats:, :] = got_ref[feats:, :]


def combine_kernel(scale, me_ref, own_ref, *refs):
    out_ref, weight_ref, terms_ref = refs[-3:]
    places = refs[:-3]
    planes = len(places)
    feats, hidden = weight_ref.shape
    low, nodes = terms_ref.shape[1:]
    half = planes // 2
    out_ref[...] = own_ref[...] + (
        places[planes - half][:feats, :].astype(F32) + places[half - 1][:feats, :].astype(F32)
    )
    for d, ref in enumerate(places):
        terms_ref[(me_ref[1] + d) % planes] = ref[feats:, :].astype(F32)
    total = terms_ref[0]
    for z in range(1, planes):
        total = total + terms_ref[z]
    total = total * scale
    lanes = 128
    per = feats // low
    for h in range(hidden // lanes):
        for g in range(per):
            start = (h * per + g) * lanes
            weight_ref[g * low:(g + 1) * low, h * lanes:(h + 1) * lanes] = total[:, start:start + lanes]


def pairwise(value, axes):
    for name, size in axes:
        bit = 1
        while bit < size:
            value = value + lax.ppermute(value, name, [(i, i ^ bit) for i in range(size)])
            bit *= 2
    return value


def per_device(embed, weight, cotangent, edge_masks, tile_rows, tile_owner, tile_sub):
    feats, nodes = embed.shape
    tiles, width, _ = edge_masks.shape
    blocks = nodes // width
    n_x, n_z, n_y = (lax.axis_size(name) for name in ("x", "z", "y_lo"))
    plane = ("x", "y_lo")
    peers = n_x * n_y
    slots = peers * n_z * 2
    hidden = weight.shape[1]
    shape = jax.ShapeDtypeStruct
    swap = functools.partial(lax.all_to_all, split_axis=0, concat_axis=0, tiled=True)

    held = swap(jnp.broadcast_to(embed[None], (n_z, feats, nodes)), "z")
    me = jnp.stack([lax.axis_index("x") * n_y + lax.axis_index("y_lo"), lax.axis_index("z")])
    me = me.astype(jnp.int32)
    ask, slot = pl.pallas_call(
        functools.partial(slots_kernel, n_z, n_y),
        out_shape=(shape((peers, slots), jnp.int32), shape((1, tiles), jnp.int32)),
        in_specs=[SM, VM, VM, VM],
        out_specs=(VM, VM),
        compiler_params=params(4),
        name="slots",
    )(me, tile_owner, tile_owner.reshape(1, tiles), tile_sub.reshape(tiles, 1))
    slot = slot.reshape(tiles)
    mine = jnp.concatenate([cotangent, weight], axis=1)
    n_feat = hidden // feats
    parts = [mine] + [
        lax.ppermute(mine, FEAT, [(i, i ^ m) for i in range(n_feat)]) for m in range(1, n_feat)
    ]
    want = pairwise(ask, (("y_lo", n_y), ("x", n_x)))

    part = lax.axis_index(FEAT).astype(jnp.int32).reshape(1)
    full = pl.pallas_call(
        order_kernel,
        out_shape=shape((hidden, nodes + hidden), BF16),
        in_specs=[SM] + [VM] * n_feat,
        out_specs=VM,
        compiler_params=params(4),
        name="order",
    )(part, *parts)
    held, full, part = lax.optimization_barrier((held, full, part))
    send = pl.pallas_call(
        select_kernel,
        out_shape=shape((slots, feats, width), BF16),
        in_specs=[SM, SM, VM],
        out_specs=VM,
        compiler_params=params(8),
        cost_estimate=cost(0, 2 * slots * feats * width * 2),
        name="select",
    )(me, want, held)
    got = swap(send, plane)

    agg, root = pl.pallas_call(
        forward_kernel,
        out_shape=(shape((feats, nodes), BF16), shape((blocks, 8, width), F32)),
        in_specs=[SM, SM, VM, VM, VM],
        out_specs=(VM, VM),
        scratch_shapes=[pltpu.VMEM((blocks, feats + 8, width), F32)],
        compiler_params=params(16),
        cost_estimate=cost(2 * tiles * feats * width * width, 2 * tiles * (feats + width) * width),
        name="forward",
    )(slot, tile_rows, got, edge_masks, embed)

    agg_full = lax.all_gather(agg, FEAT, axis=0, tiled=True)
    out, grad, scaled, terms = pl.pallas_call(
        dense_kernel,
        out_shape=(
            shape((feats, nodes), BF16),
            shape((feats, nodes), F32),
            shape((blocks, feats, width), BF16),
            shape((feats, hidden), F32),
        ),
        in_specs=[SM] + [VM] * 5,
        out_specs=(VM, VM, VM, VM),
        scratch_shapes=[pltpu.VMEM((hidden, 2 * width), F32)],
        compiler_params=params(16),
        cost_estimate=cost(
            2 * hidden * (hidden + 2 * feats) * nodes, 2 * hidden * nodes * 3, hidden * nodes
        ),
        name="dense",
    )(part, agg_full, agg, full, weight, root)

    extra = feats * hidden // width
    send_back = pl.pallas_call(
        backward_kernel,
        out_shape=shape((peers, 2 * n_z * feats + extra, width), BF16),
        in_specs=[SM, SM, VM, VM, VM],
        out_specs=VM,
        compiler_params=params(12),
        cost_estimate=cost(2 * tiles * feats * width * width, 2 * tiles * (feats + width) * width),
        name="backward",
    )(slot, tile_rows, scaled, edge_masks, terms)
    got_back = swap(send_back, plane)

    half = n_z // 2
    low = feats * hidden // nodes
    message = shape((feats + low, nodes), BF16)
    plain = shape((feats, nodes), F32)
    up, down = pl.pallas_call(
        functools.partial(start_kernel, n_z),
        out_shape=(message, message),
        in_specs=[SM, SM, VM],
        out_specs=(VM, VM),
        scratch_shapes=[pltpu.VMEM((2, blocks, feats, width), F32)],
        compiler_params=params(8),
        cost_estimate=cost(slots * feats * width // 4, slots * feats * width),
        name="start",
    )(me, want, got_back)
    sums = pl.pallas_call(
        functools.partial(gather_kernel, n_z),
        out_shape=[plain] * (n_z - 2),
        in_specs=[SM, SM, VM, VM],
        out_specs=[VM] * (n_z - 2),
        scratch_shapes=[pltpu.VMEM((n_z - 2, blocks, feats, width), F32)],
        compiler_params=params(16),
        cost_estimate=cost(slots * feats * width, 4 * slots * feats * width),
        name="gather",
    )(me, want, got_back, grad)
    sums = [*sums[:half], None, None, *sums[half:]]
    onward = [(i, (i + 1) % n_z) for i in range(n_z)]
    back = [(i, (i - 1) % n_z) for i in range(n_z)]
    places = [up] * n_z
    for hop in range(half):
        up = lax.ppermute(up, "z", onward)
        places[n_z - 1 - hop] = up
        if hop == half - 1:
            break
        down = lax.ppermute(down, "z", back)
        places[hop + 1] = down
        if hop < half - 2:
            up, down = pl.pallas_call(
                hop_kernel,
                out_shape=(message, message),
                in_specs=[VM] * 4,
                out_specs=(VM, VM),
                compiler_params=params(4),
                name="hop",
            )(up, down, sums[half - 1 - hop], sums[half + 2 + hop])
        else:
            up = pl.pallas_call(
                hop_kernel,
                out_shape=message,
                in_specs=[VM] * 2,
                out_specs=VM,
                compiler_params=params(4),
                name="hop",
            )(up, sums[half - 1 - hop])
    embed_grad, weight_grad = pl.pallas_call(
        functools.partial(combine_kernel, 1.0 / math.sqrt(nodes * n_x * n_z * n_y)),
        out_shape=(plain, shape((feats, hidden), F32)),
        in_specs=[SM] + [VM] * (1 + n_z),
        out_specs=(VM, VM),
        scratch_shapes=[pltpu.VMEM((n_z, low, nodes), F32)],
        compiler_params=params(8),
        cost_estimate=cost(3 * feats * nodes, 16 * feats * nodes),
        name="combine",
    )(me, sums[0], *places)
    return (out, embed_grad, weight_grad)


def solution(mesh):
    n_dom, n_feat = mesh.devices.shape
    wide = Mesh(mesh.devices.reshape(n_dom // 16, 8, 2, n_feat), ("x", "z", "y_lo", FEAT))
    dom = ("x", "z", "y_lo")
    in_specs = (
        P(FEAT, dom),
        P(FEAT, None),
        P(FEAT, dom),
        P(dom, None, None),
        P(dom),
        P(dom, None),
        P(dom),
    )
    out_specs = (P(FEAT, dom), P(FEAT, dom), P(FEAT, None))
    return jax.shard_map(
        per_device, mesh=wide, in_specs=in_specs, out_specs=out_specs, check_vma=False
    )
```

```python
import functools
import math

import jax
import jax.numpy as jnp
from jax import lax
from jax.experimental import pallas as pl
from jax.experimental.pallas import tpu as pltpu
from jax.sharding import Mesh, PartitionSpec as P

F32 = jnp.float32
BF16 = jnp.bfloat16
FEAT = "feat"
VM = pl.BlockSpec(memory_space=pltpu.VMEM)
SM = pl.BlockSpec(memory_space=pltpu.SMEM)


def params(mib):
    return pltpu.CompilerParams(vmem_limit_bytes=mib << 20)


def cost(flops, moved, exps=0):
    return pl.CostEstimate(flops=flops, bytes_accessed=moved, transcendentals=exps)


def slots_kernel(z_size, y_size, me_ref, owner_ref, across_ref, sub_ref, ask_ref, slot_ref):
    tiles = owner_ref.shape[0]

    def place(owner, before):
        y = owner % y_size
        z = (owner // y_size) % z_size
        x = owner // (y_size * z_size)
        return ((x * y_size + y) * z_size + z) * 2 + before

    down = lax.broadcasted_iota(jnp.int32, (tiles, tiles), 0)
    right = lax.broadcasted_iota(jnp.int32, (tiles, tiles), 1)
    same = owner_ref[...] == across_ref[...]
    before = jnp.sum((same & (right < down)).astype(jnp.int32), axis=1, keepdims=True)
    before_across = jnp.sum((same & (down < right)).astype(jnp.int32), axis=0, keepdims=True)
    slot_ref[...] = place(across_ref[...], before_across)
    lane = lax.broadcasted_iota(jnp.int32, (tiles, ask_ref.shape[1]), 1)
    asked = jnp.where(lane == place(owner_ref[...], before), sub_ref[...], 0)
    row = lax.broadcasted_iota(jnp.int32, ask_ref.shape, 0)
    ask_ref[...] = jnp.where(row == me_ref[0], jnp.sum(asked, axis=0, keepdims=True), 0)


def select_kernel(me_ref, want_ref, *refs):
    send_ref = refs[-1]
    held = refs[:-1]
    readers = want_ref.shape[0]
    owners = len(held)
    width = send_ref.shape[2]
    base = me_ref[0] * (2 * owners)

    def body(reader, carry):
        for d, ref in enumerate(held):
            z = (me_ref[1] + d) % owners
            for k in range(2):
                start = pl.multiple_of(want_ref[reader, base + 2 * z + k] * width, width)
                send_ref[(reader * owners + z) * 2 + k] = ref[:, pl.ds(start, width)]
        return carry

    lax.fori_loop(0, readers, body, 0)


def forward_kernel(slot_ref, rows_ref, got_ref, edge_ref, own_ref, agg_ref, root_ref, acc_ref):
    tiles, width, _ = edge_ref.shape
    blocks = acc_ref.shape[0]
    feats = got_ref.shape[1]
    acc_ref[...] = jnp.zeros_like(acc_ref)
    group = 8
    ones = jnp.ones((16, width), BF16)

    def body(step, carry):
        terms = []
        for j in range(group):
            tile = step * group + j
            mask = edge_ref[tile].astype(F32).astype(BF16)
            left = jnp.concatenate([got_ref[slot_ref[tile]], ones], axis=0)
            terms.append(
                lax.dot_general(left, mask, (((1,), (1,)), ((), ())), preferred_element_type=F32)
            )
        for j in range(group):
            row = rows_ref[step * group + j]
            acc_ref[row] = acc_ref[row] + terms[j][:feats + 8]
        return carry

    lax.fori_loop(0, tiles // group, body, 0)
    for r in range(blocks):
        cols = slice(r * width, (r + 1) * width)
        root = 1.0 / jnp.sqrt(1.0 + acc_ref[r, feats:feats + 8, :])
        root_ref[r] = root
        agg_ref[:, cols] = (
            own_ref[:, cols].astype(F32) + acc_ref[r, :feats, :] * root[0:1, :]
        ).astype(BF16)


def order_kernel(part_ref, *refs):
    full_ref = refs[-1]
    for m, ref in enumerate(refs[:-1]):
        feats = ref.shape[0]
        start = pl.multiple_of((part_ref[0] ^ m) * feats, feats)
        full_ref[pl.ds(start, feats), :] = ref[...]


def dense_kernel(
    part_ref, agg_ref, aggown_ref, full_ref, weight_ref, root_ref,
    out_ref, grad_ref, scaled_ref, terms_ref, act_ref,
):
    nodes = agg_ref.shape[1]
    feats = weight_ref.shape[0]
    width = scaled_ref.shape[2]
    first = pl.multiple_of(part_ref[0] * feats, feats)
    chunk = 2 * width
    terms = jnp.zeros(terms_ref.shape, F32)
    for c in range(nodes // chunk):
        cols = slice(c * chunk, (c + 1) * chunk)
        pre = lax.dot_general(
            full_ref[:, nodes:], agg_ref[:, cols], (((0,), (0,)), ((), ())), preferred_element_type=F32
        )
        gate = jax.nn.sigmoid(pre)
        act_ref[...] = pre * gate
        out_ref[:, cols] = act_ref[pl.ds(first, feats), :].astype(BF16)
        grad_pre = (full_ref[:, cols].astype(F32) * gate * (1.0 + pre * (1.0 - gate))).astype(BF16)
        grad = jnp.dot(weight_ref[...], grad_pre, preferred_element_type=F32)
        grad_ref[:, cols] = grad
        terms = terms + lax.dot_general(
            aggown_ref[:, cols], grad_pre, (((1,), (1,)), ((), ())), preferred_element_type=F32
        )
        for k in range(2):
            r = 2 * c + k
            scaled_ref[r] = (grad[:, k * width:(k + 1) * width] * root_ref[r, 0:1, :]).astype(BF16)
    terms_ref[...] = terms


def backward_kernel(slot_ref, rows_ref, scaled_ref, edge_ref, terms_ref, send_ref):
    tiles = edge_ref.shape[0]
    feats, hidden = terms_ref.shape
    width = send_ref.shape[2]
    end = send_ref.shape[1] - feats * hidden // width
    per_peer = end // feats
    group = 8
    send_ref[:, :end, :] = jnp.zeros((send_ref.shape[0], end, width), BF16)

    def body(step, carry):
        for j in range(group):
            tile = step * group + j
            slot = slot_ref[tile]
            start = pl.multiple_of((slot % per_peer) * feats, feats)
            send_ref[slot // per_peer, pl.ds(start, feats), :] = jnp.dot(
                scaled_ref[rows_ref[tile]],
                edge_ref[tile].astype(F32).astype(BF16),
                preferred_element_type=F32,
            ).astype(BF16)
        return carry

    lax.fori_loop(0, tiles // group, body, 0)
    for h in range(hidden // width):
        part = terms_ref[:, h * width:(h + 1) * width].astype(BF16)
        for p in range(send_ref.shape[0]):
            send_ref[p, end + h * feats:end + (h + 1) * feats, :] = part


def add_up(distances, me_ref, want_ref, got_ref, acc_ref, owners):
    _, blocks, feats, width = acc_ref.shape
    readers = want_ref.shape[0]
    base = me_ref[0] * (2 * owners)

    def body(reader, carry):
        for i, d in enumerate(distances):
            z = (me_ref[1] + d) % owners
            for k in range(2):
                block = want_ref[reader, base + 2 * z + k]
                start = pl.multiple_of((2 * z + k) * feats, feats)
                acc_ref[i, block] = acc_ref[i, block] + got_ref[reader, pl.ds(start, feats), :].astype(F32)
        return carry

    lax.fori_loop(0, readers, body, 0)


def start_kernel(owners, me_ref, want_ref, got_ref, up_ref, down_ref, acc_ref):
    _, blocks, feats, width = acc_ref.shape
    half = owners // 2
    acc_ref[...] = jnp.zeros_like(acc_ref)
    add_up((half, half + 1), me_ref, want_ref, got_ref, acc_ref, owners)
    end = 2 * owners * feats
    low = up_ref.shape[0] - feats
    for h in range((got_ref.shape[1] - end) // low):
        rows = slice(end + h * low, end + (h + 1) * low)
        terms = got_ref[0, rows, :].astype(F32)
        for q in range(1, got_ref.shape[0]):
            terms = terms + got_ref[q, rows, :].astype(F32)
        up_ref[feats:, h * width:(h + 1) * width] = terms.astype(BF16)
        down_ref[feats:, h * width:(h + 1) * width] = terms.astype(BF16)
    for i, ref in enumerate((up_ref, down_ref)):
        for r in range(blocks):
            ref[:feats, r * width:(r + 1) * width] = acc_ref[i, r].astype(BF16)


def gather_kernel(owners, me_ref, want_ref, got_ref, grad_ref, *refs):
    acc_ref = refs[-1]
    _, blocks, feats, width = acc_ref.shape
    half = owners // 2
    acc_ref[...] = jnp.zeros_like(acc_ref)
    for r in range(blocks):
        acc_ref[0, r] = grad_ref[:, r * width:(r + 1) * width]
    distances = [d for d in range(owners) if d not in (half, half + 1)]
    add_up(distances, me_ref, want_ref, got_ref, acc_ref, owners)
    for i, ref in enumerate(refs[:-1]):
        for r in range(blocks):
            ref[:, r * width:(r + 1) * width] = acc_ref[i, r]


def hop_kernel(*refs):
    many = len(refs) // 3
    for got_ref, sum_ref, on_ref in zip(refs[:many], refs[many:2 * many], refs[2 * many:]):
        feats = sum_ref.shape[0]
        on_ref[:feats, :] = (got_ref[:feats, :].astype(F32) + sum_ref[...]).astype(BF16)
        on_ref[feats:, :] = got_ref[feats:, :]


def combine_kernel(scale, me_ref, own_ref, *refs):
    out_ref, weight_ref, terms_ref = refs[-3:]
    places = refs[:-3]
    planes = len(places)
    feats, hidden = weight_ref.shape
    low, nodes = terms_ref.shape[1:]
    half = planes // 2
    out_ref[...] = own_ref[...] + (
        places[planes - half][:feats, :].astype(F32) + places[half - 1][:feats, :].astype(F32)
    )
    for d, ref in enumerate(places):
        terms_ref[(me_ref[1] + d) % planes] = ref[feats:, :].astype(F32)
    total = terms_ref[0]
    for z in range(1, planes):
        total = total + terms_ref[z]
    total = total * scale
    lanes = 128
    per = feats // low
    for h in range(hidden // lanes):
        for g in range(per):
            start = (h * per + g) * lanes
            weight_ref[g * low:(g + 1) * low, h * lanes:(h + 1) * lanes] = total[:, start:start + lanes]


def pairwise(value, axes):
    for name, size in axes:
        bit = 1
        while bit < size:
            value = value + lax.ppermute(value, name, [(i, i ^ bit) for i in range(size)])
            bit *= 2
    return value


def per_device(embed, weight, cotangent, edge_masks, tile_rows, tile_owner, tile_sub):
    feats, nodes = embed.shape
    tiles, width, _ = edge_masks.shape
    blocks = nodes // width
    n_x, n_z, n_y = (lax.axis_size(name) for name in ("x", "z", "y_lo"))
    plane = ("x", "y_lo")
    peers = n_x * n_y
    slots = peers * n_z * 2
    hidden = weight.shape[1]
    shape = jax.ShapeDtypeStruct
    swap = functools.partial(lax.all_to_all, split_axis=0, concat_axis=0, tiled=True)

    me = jnp.stack([lax.axis_index("x") * n_y + lax.axis_index("y_lo"), lax.axis_index("z")])
    me = me.astype(jnp.int32)
    ask, slot = pl.pallas_call(
        functools.partial(slots_kernel, n_z, n_y),
        out_shape=(shape((peers, slots), jnp.int32), shape((1, tiles), jnp.int32)),
        in_specs=[SM, VM, VM, VM],
        out_specs=(VM, VM),
        compiler_params=params(4),
        name="slots",
    )(me, tile_owner, tile_owner.reshape(1, tiles), tile_sub.reshape(tiles, 1))
    slot = slot.reshape(tiles)
    mine = jnp.concatenate([cotangent, weight], axis=1)
    n_feat = hidden // feats
    parts = [mine] + [
        lax.ppermute(mine, FEAT, [(i, i ^ m) for i in range(n_feat)]) for m in range(1, n_feat)
    ]
    onward = [(i, (i + 1) % n_z) for i in range(n_z)]
    back = [(i, (i - 1) % n_z) for i in range(n_z)]
    half = n_z // 2
    held = [embed] * n_z
    up = down = embed
    steps = [("y_lo", n_y, 1), ("x", n_x, 1), ("x", n_x, 2)]
    for hop in range(half):
        up = lax.ppermute(up, "z", onward)
        if hop < half - 1:
            down = lax.ppermute(down, "z", back)
        if hop < len(steps):
            name, size, bit = steps[hop]
            ask = ask + lax.ppermute(ask, name, [(i, i ^ bit) for i in range(size)])
        if hop < half - 1:
            if hop == 1:
                up, down, ask, *parts = lax.optimization_barrier((up, down, ask, *parts))
            else:
                up, down, ask = lax.optimization_barrier((up, down, ask))
        held[n_z - 1 - hop] = up
        if hop < half - 1:
            held[hop + 1] = down
    want = ask

    part = lax.axis_index(FEAT).astype(jnp.int32).reshape(1)
    full = pl.pallas_call(
        order_kernel,
        out_shape=shape((hidden, nodes + hidden), BF16),
        in_specs=[SM] + [VM] * n_feat,
        out_specs=VM,
        compiler_params=params(4),
        name="order",
    )(part, *parts)
    held, full, part = lax.optimization_barrier((held, full, part))
    send = pl.pallas_call(
        select_kernel,
        out_shape=shape((slots, feats, width), BF16),
        in_specs=[SM, SM] + [VM] * n_z,
        out_specs=VM,
        compiler_params=params(8),
        cost_estimate=cost(0, 2 * slots * feats * width * 2),
        name="select",
    )(me, want, *held)
    got = swap(send, plane)

    agg, root = pl.pallas_call(
        forward_kernel,
        out_shape=(shape((feats, nodes), BF16), shape((blocks, 8, width), F32)),
        in_specs=[SM, SM, VM, VM, VM],
        out_specs=(VM, VM),
        scratch_shapes=[pltpu.VMEM((blocks, feats + 8, width), F32)],
        compiler_params=params(16),
        cost_estimate=cost(2 * tiles * feats * width * width, 2 * tiles * (feats + width) * width),
        name="forward",
    )(slot, tile_rows, got, edge_masks, embed)

    agg_full = lax.all_gather(agg, FEAT, axis=0, tiled=True)
    out, grad, scaled, terms = pl.pallas_call(
        dense_kernel,
        out_shape=(
            shape((feats, nodes), BF16),
            shape((feats, nodes), F32),
            shape((blocks, feats, width), BF16),
            shape((feats, hidden), F32),
        ),
        in_specs=[SM] + [VM] * 5,
        out_specs=(VM, VM, VM, VM),
        scratch_shapes=[pltpu.VMEM((hidden, 2 * width), F32)],
        compiler_params=params(16),
        cost_estimate=cost(
            2 * hidden * (hidden + 2 * feats) * nodes, 2 * hidden * nodes * 3, hidden * nodes
        ),
        name="dense",
    )(part, agg_full, agg, full, weight, root)

    extra = feats * hidden // width
    send_back = pl.pallas_call(
        backward_kernel,
        out_shape=shape((peers, 2 * n_z * feats + extra, width), BF16),
        in_specs=[SM, SM, VM, VM, VM],
        out_specs=VM,
        compiler_params=params(12),
        cost_estimate=cost(2 * tiles * feats * width * width, 2 * tiles * (feats + width) * width),
        name="backward",
    )(slot, tile_rows, scaled, edge_masks, terms)
    got_back = swap(send_back, plane)

    low = feats * hidden // nodes
    message = shape((feats + low, nodes), BF16)
    plain = shape((feats, nodes), F32)
    up, down = pl.pallas_call(
        functools.partial(start_kernel, n_z),
        out_shape=(message, message),
        in_specs=[SM, SM, VM],
        out_specs=(VM, VM),
        scratch_shapes=[pltpu.VMEM((2, blocks, feats, width), F32)],
        compiler_params=params(8),
        cost_estimate=cost(slots * feats * width // 4, slots * feats * width),
        name="start",
    )(me, want, got_back)
    sums = pl.pallas_call(
        functools.partial(gather_kernel, n_z),
        out_shape=[plain] * (n_z - 2),
        in_specs=[SM, SM, VM, VM],
        out_specs=[VM] * (n_z - 2),
        scratch_shapes=[pltpu.VMEM((n_z - 2, blocks, feats, width), F32)],
        compiler_params=params(16),
        cost_estimate=cost(slots * feats * width, 4 * slots * feats * width),
        name="gather",
    )(me, want, got_back, grad)
    sums = [*sums[:half], None, None, *sums[half:]]
    places = [up] * n_z
    for hop in range(half):
        up = lax.ppermute(up, "z", onward)
        places[n_z - 1 - hop] = up
        if hop == half - 1:
            break
        down = lax.ppermute(down, "z", back)
        places[hop + 1] = down
        if hop < half - 2:
            up, down = pl.pallas_call(
                hop_kernel,
                out_shape=(message, message),
                in_specs=[VM] * 4,
                out_specs=(VM, VM),
                compiler_params=params(4),
                name="hop",
            )(up, down, sums[half - 1 - hop], sums[half + 2 + hop])
        else:
            up = pl.pallas_call(
                hop_kernel,
                out_shape=message,
                in_specs=[VM] * 2,
                out_specs=VM,
                compiler_params=params(4),
                name="hop",
            )(up, sums[half - 1 - hop])
    embed_grad, weight_grad = pl.pallas_call(
        functools.partial(combine_kernel, 1.0 / math.sqrt(nodes * n_x * n_z * n_y)),
        out_shape=(plain, shape((feats, hidden), F32)),
        in_specs=[SM] + [VM] * (1 + n_z),
        out_specs=(VM, VM),
        scratch_shapes=[pltpu.VMEM((n_z, low, nodes), F32)],
        compiler_params=params(8),
        cost_estimate=cost(3 * feats * nodes, 16 * feats * nodes),
        name="combine",
    )(me, sums[0], *places)
    return (out, embed_grad, weight_grad)


def solution(mesh):
    n_dom, n_feat = mesh.devices.shape
    wide = Mesh(mesh.devices.reshape(n_dom // 16, 8, 2, n_feat), ("x", "z", "y_lo", FEAT))
    dom = ("x", "z", "y_lo")
    in_specs = (
        P(FEAT, dom),
        P(FEAT, None),
        P(FEAT, dom),
        P(dom, None, None),
        P(dom),
        P(dom, None),
        P(dom),
    )
    out_specs = (P(FEAT, dom), P(FEAT, dom), P(FEAT, None))
    return jax.shard_map(
        per_device, mesh=wide, in_specs=in_specs, out_specs=out_specs, check_vma=False
    )
```
